256 devices in a mesh: dp: 64 (over x, z, y_lo), seq: 4 (over y_hi, core).
Axes of the slice: x: 4, y: 4 (y_hi: 2, y_lo: 2; y = y_hi * 2 + y_lo), z: 8, core: 2. Of those that a mesh axis runs over, the one named last changes fastest.
Arguments:
- block_input: float32 [128, 512, 768], P('dp', 'seq'), may hold values from -6 to 6
- doc_ids: int32 [128, 512], P('dp'), may hold values from 0 to 2, as said below
- positions: int32 [128, 512], P('dp', 'seq'), may hold values from 0 to 509, as said below
- w_qkv: bfloat16 [768, 2304], P(('dp', 'seq')), may hold values from -0.21875 to 0.21875
- w_out: bfloat16 [768, 768], P(('dp', 'seq')), may hold values from -2.5 to 2.5
- w_in: bfloat16 [768, 2304], P(('dp', 'seq')), may hold values from -0.21875 to 0.21875
- w_down: bfloat16 [768, 1152], P(('dp', 'seq')), may hold values from -0.1875 to 0.1875
- gain_attn: bfloat16 [768], P(('dp', 'seq')), may hold values from 0.099609375 to 1.8984375
- gain_ffn: bfloat16 [768], P(('dp', 'seq')), may hold values from 0.099609375 to 1.8984375
- cotangent: float32 [128, 512, 768], P('dp', 'seq'), may hold values from -16 to 16
Outputs:
- block_output: float32 [128, 512, 768], P('dp', 'seq')
- input_grad: float32 [128, 512, 768], P('dp', 'seq')
- grad_qkv: float32 [768, 2304], P(('dp', 'seq'))
- grad_out: float32 [768, 768], P(('dp', 'seq'))
- grad_in: float32 [768, 2304], P(('dp', 'seq'))
- grad_down: float32 [768, 1152], P(('dp', 'seq'))
- grad_gain_attn: float32 [768], P(('dp', 'seq'))
- grad_gain_ffn: float32 [768], P(('dp', 'seq'))
The draws below stay inside these ranges and needn't reach their ends.
Inputs may be any that keep to these rules, and one draw needn't show every extreme that they name: `doc_ids`: every sequence holds exactly 3 documents, each a run of tokens, with ids 0 to 2 in order; the boundaries differ from sequence to sequence. `positions`: a token's position counted from the first token of its document.
All inputs are finite; a program needn't handle non-finite values.
Results may differ from the reference program's by a relative error of at most 0.02.
Values may be sent and summed in bfloat16 or wider, within the bound.
A program may use at most 128 MiB of HBM per device.

```python
import jax
import jax.numpy as jnp
from jax import lax

D = 768
H = 12
HD = 64
FF = 1152
LEN = 512
DOCS = 3
NSEQ = 128


def doc_layout(key):
    span = LEN // (DOCS - 1)
    cuts = jax.random.randint(jax.random.fold_in(key, 202), (NSEQ, DOCS - 1), 1, span) + jnp.arange(DOCS - 1, dtype=jnp.int32) * span
    cuts = cuts.at[0, 0].set(1).at[0, 1].set(2 * span - 1)
    where_now = jnp.arange(LEN, dtype=jnp.int32)
    passed = where_now[None, :, None] >= cuts[:, None, :]
    doc_number = jnp.sum(passed.astype(jnp.int32), axis=-1)
    begins = jnp.max(jnp.where(passed, cuts[:, None, :], 0), axis=-1)
    return (doc_number.astype(jnp.int32), (where_now[None, :] - begins).astype(jnp.int32))


def draw_doc_ids(key, part):
    return doc_layout(key)[0]


def draw_positions(key, part):
    return doc_layout(key)[1]


def with_spikes(array, own_key, source, target, blocks, factor):
    def block_of(axis_at):
        return (jnp.arange(array.shape[axis_at]) // (array.shape[axis_at] // blocks)).reshape((-1,) + (1,) * (array.ndim - 1 - axis_at))

    first = jax.random.permutation(own_key, blocks)[block_of(target)]
    second = (block_of(target) + blocks // 2) % blocks
    return jnp.where((block_of(source) == first) | (block_of(source) == second), factor * array, array)


def shard_levels(key, shape, pieces, low, top_value):
    def one(dim, blocks):
        draws = jax.random.uniform(jax.random.fold_in(jax.random.fold_in(key, 6), dim), (blocks,), jnp.float32, low / len(pieces), top_value / len(pieces))
        return jnp.repeat(jnp.exp(draws), shape[dim] // blocks).reshape((-1,) + (1,) * (len(shape) - dim - 1))

    level = one(*pieces[0])
    for cut in pieces[1:]:
        level = level * one(*cut)
    return level


def centred(key, dims, scale, bound, split=(), kind=jnp.bfloat16):
    entries = jax.random.normal(key, dims, jnp.float32) * scale
    if len(split) > 0:
        entries = shard_levels(key, dims, split, -0.22, 0.18) * entries
    return jnp.clip(entries, min=-bound, max=bound).astype(kind)


def bell_draw_with(own_key, extent, deviation, bound, shards, heavy, kind=jnp.bfloat16):
    entries = deviation * jax.random.normal(own_key, extent, jnp.float32)
    if shards:
        entries = entries * shard_levels(own_key, extent, shards, -0.22, 0.18)
    return jnp.clip(with_spikes(entries, jax.random.fold_in(own_key, 3), *heavy), -bound, bound).astype(kind)


def setup_inputs(seed: int = 0) -> dict:
    splits = jax.random.split(jax.random.key(seed), 11)
    block_input = centred(splits[0], (NSEQ, LEN, D), 1.0, 6.0, ((0, 64), (1, 4)), jnp.float32)
    doc_ids = draw_doc_ids(jax.random.fold_in(splits[10], 71), 0)
    positions = draw_positions(jax.random.fold_in(splits[10], 71), 0)
    w_qkv = centred(splits[3], (D, 3 * D), D ** -0.5, 0.21875, ((0, 256),))
    w_out = centred(splits[4], (D, D), (D // 128) ** -0.5, 2.5, ((0, 256),))
    w_in = centred(splits[5], (D, 2 * FF), D ** -0.5, 0.21875, ((0, 256),))
    w_down = centred(splits[6], (D, FF), FF ** -0.5, 0.1875, ((0, 256),))
    gain_attn = jnp.clip(1.0 + 0.18 * jax.random.normal(splits[7], (D,), jnp.float32), 0.099609375, 1.8984375).astype(jnp.bfloat16)
    gain_ffn = jnp.clip(1.0 + 0.18 * jax.random.normal(splits[8], (D,), jnp.float32), 0.099609375, 1.8984375).astype(jnp.bfloat16)
    cotangent = bell_draw_with(splits[9], (NSEQ, LEN, D), 1.0, 16.0, ((0, 64), (1, 4)), (0, 2, 64, 4.0), jnp.float32)
    return {"block_input": block_input, "doc_ids": doc_ids, "positions": positions, "w_qkv": w_qkv, "w_out": w_out, "w_in": w_in, "w_down": w_down, "gain_attn": gain_attn, "gain_ffn": gain_ffn, "cotangent": cotangent}


norm_eps = 1e-05
rope_base = 160000.0

def normalize(matrix):
    center = matrix - lax.optimization_barrier(jnp.mean(matrix, axis=-1, keepdims=True))
    inverse = lax.rsqrt(lax.optimization_barrier(jnp.mean(center * center, axis=-1, keepdims=True)) + norm_eps)
    return (center * inverse, inverse)

def norm_back(grad_hat, normed, inverse):
    first_mean = lax.optimization_barrier(jnp.mean(grad_hat, axis=-1, keepdims=True))
    cross_mean = lax.optimization_barrier(jnp.mean(grad_hat * normed, axis=-1, keepdims=True))
    return (grad_hat - first_mean - normed * cross_mean) * inverse

def rotary_tables(pos_row):
    half_dim = HD // 2
    frequency = rope_base ** (-(jnp.arange(half_dim).astype(jnp.float32) * (2.0 / HD)))
    angles = pos_row.astype(jnp.float32)[:, None] * frequency[None, :]
    return (jnp.cos(angles)[:, None, :], jnp.sin(angles)[:, None, :])

def rotate(matrix, cosine, sine_part):
    half_dim = HD // 2
    first_half = matrix[..., :half_dim]
    second_half = matrix[..., half_dim:]
    return jnp.concatenate([first_half * cosine - second_half * sine_part, second_half * cosine + first_half * sine_part], axis=-1)

def unrotate(matrix, cosine, sine_part):
    half_dim = HD // 2
    first_half = matrix[..., :half_dim]
    second_half = matrix[..., half_dim:]
    return jnp.concatenate([first_half * cosine + second_half * sine_part, second_half * cosine - first_half * sine_part], axis=-1)

def gelu_pair(gate_half):
    normal_cdf = 0.5 * (1.0 + lax.erf(gate_half * 0.7071067811865476))
    density = jnp.exp(-0.5 * gate_half * gate_half) * 0.3989422804014327
    return (gate_half * normal_cdf, normal_cdf + gate_half * density)

def one_sequence(weights, tokens, doc_row, pos_row, grad_top):
    w_qkv, w_out, w_in, w_down, gain_attn, gain_ffn = weights
    length = tokens.shape[0]
    score_scale = HD ** (-0.5)
    normed_one, inverse_one = normalize(tokens)
    input_one = (normed_one * gain_attn.astype(jnp.float32)).astype(jnp.bfloat16)
    packed = jnp.dot(input_one, w_qkv, preferred_element_type=jnp.float32)
    cosine, sine_part = rotary_tables(pos_row)
    queries = rotate(packed[:, :D].reshape(length, H, HD), cosine, sine_part).astype(jnp.bfloat16)
    key_rows = rotate(packed[:, D:2 * D].reshape(length, H, HD), cosine, sine_part).astype(jnp.bfloat16)
    value_rows = packed[:, 2 * D:].reshape(length, H, HD).astype(jnp.bfloat16)
    same_doc = (doc_row[:, None] == doc_row[None, :])[None]
    scores = jnp.einsum('qhd,khd->hqk', queries.astype(jnp.float32), key_rows.astype(jnp.float32)) * score_scale
    masked = jnp.where(same_doc, scores, -jnp.inf)
    row_top = lax.optimization_barrier(jnp.max(masked, axis=-1, keepdims=True))
    log_total = row_top + jnp.log(lax.optimization_barrier(jnp.sum(jnp.exp(masked - row_top), axis=-1, keepdims=True)))
    soft_full = jnp.exp(masked - log_total)
    soft_low = soft_full.astype(jnp.bfloat16)
    mixed_heads = jnp.einsum('hqk,khd->qhd', soft_low.astype(jnp.float32), value_rows.astype(jnp.float32))
    attended = mixed_heads.reshape(length, D).astype(jnp.bfloat16)
    residual = tokens + jnp.dot(attended, w_out.T, preferred_element_type=jnp.float32)
    normed_two, inverse_two = normalize(residual)
    input_two = (normed_two * gain_ffn.astype(jnp.float32)).astype(jnp.bfloat16)
    pre_act = jnp.dot(input_two, w_in, preferred_element_type=jnp.float32)
    gate_half = pre_act[:, :FF]
    up_half = pre_act[:, FF:]
    activated, gate_slope = gelu_pair(gate_half)
    hidden = (activated * up_half).astype(jnp.bfloat16)
    block_output = residual + jnp.dot(hidden, w_down.T, preferred_element_type=jnp.float32)
    grad_low = grad_top.astype(jnp.bfloat16)
    grad_down = jnp.dot(grad_low.T, hidden, preferred_element_type=jnp.float32)
    grad_hidden = jnp.dot(grad_low, w_down, preferred_element_type=jnp.float32)
    grad_pre = jnp.concatenate([grad_hidden * up_half * gate_slope, grad_hidden * activated], axis=-1).astype(jnp.bfloat16)
    grad_in = jnp.dot(input_two.T, grad_pre, preferred_element_type=jnp.float32)
    grad_norm_two = jnp.dot(grad_pre, w_in.T, preferred_element_type=jnp.float32)
    grad_gain_ffn = lax.optimization_barrier(jnp.sum(grad_norm_two * normed_two, axis=0))
    grad_resid = grad_top + norm_back(grad_norm_two * gain_ffn.astype(jnp.float32), normed_two, inverse_two)
    resid_low = grad_resid.astype(jnp.bfloat16)
    grad_wout = jnp.dot(resid_low.T, attended, preferred_element_type=jnp.float32)
    grad_att = jnp.dot(resid_low, w_out, preferred_element_type=jnp.float32).astype(jnp.bfloat16).reshape(length, H, HD)
    row_delta = lax.optimization_barrier(jnp.sum(grad_att.astype(jnp.float32) * attended.reshape(length, H, HD).astype(jnp.float32), axis=-1)).T[:, :, None]
    grad_probs = jnp.einsum('qhd,khd->hqk', grad_att.astype(jnp.float32), value_rows.astype(jnp.float32))
    grad_scores = (soft_full * (grad_probs - row_delta) * score_scale).astype(jnp.bfloat16)
    grad_query = jnp.einsum('hqk,khd->qhd', grad_scores.astype(jnp.float32), key_rows.astype(jnp.float32))
    grad_key = jnp.einsum('hqk,qhd->khd', grad_scores.astype(jnp.float32), queries.astype(jnp.float32))
    grad_value = jnp.einsum('hqk,qhd->khd', soft_low.astype(jnp.float32), grad_att.astype(jnp.float32))
    grad_packed = jnp.concatenate([unrotate(grad_query, cosine, sine_part).reshape(length, D), unrotate(grad_key, cosine, sine_part).reshape(length, D), grad_value.reshape(length, D)], axis=-1).astype(jnp.bfloat16)
    grad_wqkv = jnp.dot(input_one.T, grad_packed, preferred_element_type=jnp.float32)
    grad_norm_one = jnp.dot(grad_packed, w_qkv.T, preferred_element_type=jnp.float32)
    grad_gain_attn = lax.optimization_barrier(jnp.sum(grad_norm_one * normed_one, axis=0))
    input_grad = grad_resid + norm_back(grad_norm_one * gain_attn.astype(jnp.float32), normed_one, inverse_one)
    return (block_output, input_grad, (grad_wqkv, grad_wout, grad_in, grad_down, grad_gain_attn, grad_gain_ffn))

def reference(block_input, doc_ids, positions, w_qkv, w_out, w_in, w_down, gain_attn, gain_ffn, cotangent):
    weights = (w_qkv, w_out, w_in, w_down, gain_attn, gain_ffn)

    def scan_step(running, inputs):
        tokens, doc_row, pos_row, grad_top = inputs
        out_row, grad_row, gradients = one_sequence(weights, tokens, doc_row, pos_row, grad_top)
        return (jax.tree.map(jnp.add, running, gradients), (out_row, grad_row))
    zero_grads = (jnp.zeros((D, 3 * D), jnp.float32), jnp.zeros((D, D), jnp.float32), jnp.zeros((D, 2 * FF), jnp.float32), jnp.zeros((D, FF), jnp.float32), jnp.zeros((D,), jnp.float32), jnp.zeros((D,), jnp.float32))
    totals, stacked = lax.scan(scan_step, zero_grads, (block_input, doc_ids, positions, cotangent))
    return (stacked[0], stacked[1], totals[0], totals[1], totals[2], totals[3], totals[4], totals[5])
```

```python
import math


import jax
import jax.numpy as jnp
from jax import lax
from jax.experimental import pallas as pl
from jax.experimental.pallas import tpu as pltpu
from jax.sharding import PartitionSpec as P

D = 768
H = 12
HD = 64
FF = 1152
NW = 6528
NC = 6656
START = (0, 2560)
WIDE = (640, 1024)
SIZE = (32, 48)
MANY = (5, 8)
CUT = (((0, 384), (384, 256)), ((0, 512), (512, 512)))
MESH = pl.DeviceIdType.MESH
f32 = jnp.float32
bf16 = jnp.bfloat16


def coords():
    dp = lax.axis_index("dp")
    sq = lax.axis_index("seq")
    x = lax.div(dp, 16)
    z = lax.rem(lax.div(dp, 2), 8)
    ylo = lax.rem(dp, 2)
    yhi = lax.div(sq, 2)
    c = lax.rem(sq, 2)
    return x, yhi * 2 + ylo, z, c


def device(x, y, z, c):
    return (x * 16 + z * 2 + lax.rem(y, 2), lax.div(y, 2) * 2 + c)


def remote(src, dst, send, recv, to):
    return pltpu.make_async_remote_copy(
        src_ref=src, dst_ref=dst, send_sem=send, recv_sem=recv, device_id=to, device_id_type=MESH
    )


def greet(x, y, z, c):
    barrier = pltpu.get_barrier_semaphore()
    peers = [device(x, y, z, 1 - c)]
    peers += [device(lax.rem(x + k, 4), y, z, c) for k in (1, 3)]
    peers += [device(x, lax.rem(y + k, 4), z, c) for k in (1, 2, 3)]
    for to in peers:
        pl.semaphore_signal(barrier, inc=1, device_id=to, device_id_type=MESH)

    def hail(k, _):
        pl.semaphore_signal(
            barrier, inc=1, device_id=device(x, y, lax.rem(z + k, 8), c), device_id_type=MESH
        )
        return 0

    lax.fori_loop(1, 8, hail, 0)
    pl.semaphore_wait(barrier, len(peers) + 7)


class Ring:
    def __init__(self, me, to, block, send, recv, first):
        self.right = lax.rem(me + 1, 4)
        self.left = lax.rem(me + 3, 4)
        self.far = lax.rem(me + 2, 4)
        self.me, self.to, self.block, self.first = me, to, block, first
        self.send, self.recv = send, recv
        self.started = []

    def go(self, slot, i, h, to, src=None):
        copy = remote(
            self.block(i, h) if src is None else src,
            self.block(i, h),
            self.send.at[slot],
            self.recv.at[slot],
            self.to(to),
        )
        copy.start()
        self.started.append(copy)

    def begin(self):
        mine = self.first
        self.go(0, self.me, 0, self.right, mine(0) if mine else None)
        self.go(1, self.me, 1, self.left, mine(1) if mine else None)
        self.go(2, self.me, 1, self.right, mine(1) if mine else None)
        self.go(3, self.me, 0, self.left, mine(0) if mine else None)

    def got(self, slot, i, h):
        remote(
            self.block(i, h), self.block(i, h), self.send.at[slot], self.recv.at[slot], self.to(self.right)
        ).wait_recv()

    def forward(self):
        self.got(0, self.left, 0)
        self.go(4, self.left, 0, self.right)
        self.got(1, self.right, 1)
        self.go(5, self.right, 1, self.left)

    def near(self):
        self.got(2, self.left, 1)
        self.got(3, self.right, 0)

    def last(self):
        self.got(4, self.far, 0)
        self.got(5, self.far, 1)

    def sent(self):
        for copy in self.started:
            copy.wait_send()


class Reduce:
    def __init__(self, me, to, block, land, send, recv):
        self.right = lax.rem(me + 1, 4)
        self.left = lax.rem(me + 3, 4)
        self.far = lax.rem(me + 2, 4)
        self.me, self.to, self.block, self.land = me, to, block, land
        self.send, self.recv = send, recv
        self.started = []

    def go(self, slot, i, h, to):
        copy = remote(
            self.block(i, h), self.land(slot, h), self.send.at[slot], self.recv.at[slot], self.to(to)
        )
        copy.start()
        self.started.append(copy)

    def got(self, slot, h):
        at = self.land(slot, h)
        remote(at, at, self.send.at[slot], self.recv.at[slot], self.to(self.right)).wait_recv()

    def one(self):
        self.go(0, self.far, 0, self.right)
        self.go(1, self.far, 1, self.left)

    def two(self):
        self.go(3, self.right, 1, self.right)

    def three(self):
        self.go(4, self.left, 0, self.left)

    def pass_right(self):
        self.got(0, 0)
        add_into(self.block(self.right, 0), self.land(0, 0))
        self.go(2, self.right, 0, self.right)

    def pass_left(self):
        self.got(1, 1)
        add_into(self.block(self.left, 1), self.land(1, 1))
        self.go(5, self.left, 1, self.left)

    def landed(self):
        for slot, h in ((3, 1), (4, 0), (2, 0), (5, 1)):
            self.got(slot, h)

    def sent(self):
        for copy in self.started:
            copy.wait_send()


def add_into(at, more):
    def row(r, _):
        at[r] = (at[r].astype(f32) + more[r].astype(f32)).astype(bf16)
        return 0

    lax.fori_loop(0, 3, row, 0)


def normalize(matrix):
    center = matrix - jnp.mean(matrix, axis=-1, keepdims=True)
    inverse = lax.rsqrt(jnp.mean(center * center, axis=-1, keepdims=True) + 1e-05)
    return center * inverse, inverse


def norm_back(grad_hat, normed, inverse):
    first_mean = jnp.mean(grad_hat, axis=-1, keepdims=True)
    cross_mean = jnp.mean(grad_hat * normed, axis=-1, keepdims=True)
    return (grad_hat - first_mean - normed * cross_mean) * inverse


def dot(left, right):
    return jnp.dot(left, right, preferred_element_type=f32)


def dot_rows(left, right):
    return lax.dot_general(left, right, (((1,), (1,)), ((), ())), preferred_element_type=f32)


def dot_over(left, right):
    return lax.dot_general(left, right, (((0,), (0,)), ((), ())), preferred_element_type=f32)


def tiles(count, width, step):
    def one(n, _):
        step(pl.ds(pl.multiple_of(n * width, width), width))
        return 0

    lax.fori_loop(0, count, one, 0)


def shifted(at, by):
    return pl.ds(pl.multiple_of(at.start + by, 128), at.size)


def block_kernel(
    blk, tok, cot, doc, r_out, o_out, g_out,
    sb_a, sb_b, sf_a, sf_b, give_x, give_g, xs, gs, w, d_w, half, land2_a, land2_b, land1_a, land1_b, zbuf_a, zbuf_b, res_a, res_b,
    d_out, d_tok, tok_half, tok_sum,
    cosine, sine, inner, tok_in, normed_all, inverse_all, in_all, q, k, v, bias, soft, att, first_part,
    normed_two, in_two, top, hidden, d_pre, d_two, back_two, resid, d_att, d_q, d_kv, d_one,
    in_all_t, in_own_t, in_two_t, resid_t, top_t, out_low,
    pair_s, pair_r, z_s, z_r, ring_s, ring_r, core_s, core_r, loc, tok_s, tok_r,
    half_s, half_r, back_s, back_r, y_s, y_r, fin_s, fin_r, ret_s, ret_r, keep_s,
):
    x, y, z, c = coords()
    hi = lax.div(y, 2)
    greet(x, y, z, c)
    sib = device(x, y, z, 1 - c)
    far = device(x, lax.rem(y + 2, 4), z, c)
    along_x = lambda i: device(i, y, z, c)
    along_y = lambda i: device(x, i, z, c)
    b_own = 2 * hi + c
    b_far = 2 * (1 - hi) + c

    sb, sf, zbuf, res = (sb_a, sb_b), (sf_a, sf_b), (zbuf_a, zbuf_b), (res_a, res_b)
    part = (pl.ds(0, 32), pl.ds(32, 48))

    def owner(g, o, n=1):
        return pl.ds(pl.multiple_of(o * SIZE[g], SIZE[g]), SIZE[g] * n)

    def cols(g, core, p, at=0, n=None):
        n = WIDE[g] if n is None else n
        return pl.ds(pl.multiple_of(START[g] + core * 2 * WIDE[g] + p * WIDE[g] + at, 128), n)

    mine, pair = [], []
    for g in range(2):
        at = sb[g].at[owner(g, z * 2 + c)]
        mine.append(pltpu.make_async_copy(blk.at[c, part[g]], at, loc.at[g]))
        mine[g].start()
        pair.append(remote(blk.at[1 - c, part[g]], at, pair_s.at[g], pair_r.at[g], sib))
        pair[g].start()

    def spread(g):
        mine[g].wait()
        pair[g].wait()
        at = sb[g].at[owner(g, z * 2, 2)]

        def push(n, _):
            remote(at, at, z_s.at[g, n], z_r.at[g, n], device(x, y, lax.rem(z + n, 8), c)).start()
            return 0

        lax.fori_loop(1, 8, push, 0)

    give_x[...] = tok[1 - hi].astype(bf16)
    give_g[...] = cot[1 - hi].astype(bf16)
    xs[b_own] = tok[hi].astype(bf16)
    gs[hi] = cot[hi].astype(bf16)
    spread(0)
    spread(1)
    give = [
        remote(give_x, xs.at[b_own], tok_s.at[0], tok_r.at[0], far),
        remote(give_g, gs.at[hi], tok_s.at[1], tok_r.at[1], far),
        remote(xs.at[b_own], xs.at[b_own], tok_s.at[2], tok_r.at[2], sib),
    ]
    for copy in give:
        copy.start()

    lane = lax.broadcasted_iota(jnp.int32, (1, 128), 1)
    low = (lane & 63) < 32
    heads = (lane < 64, lane >= 64)
    own = [pl.ds(pl.multiple_of(c * 128 + j * 256, 128), 128) for j in range(2)]
    local = [pl.ds(j * 128, 128) for j in range(2)]

    p_row = lax.broadcasted_iota(jnp.int32, (1, D), 1)
    o, gy, gx = p_row & 15, (p_row >> 4) & 3, (p_row >> 6) & 3
    holder = ((gx * 8 + (o >> 1)) * 2 + (gy & 1)) * 4 + (gy >> 1) * 2 + (o & 1)
    feature = holder * 3 + (p_row >> 8)
    inner[...] = (lax.broadcasted_iota(jnp.int32, (D, D), 0) == feature).astype(f32).astype(bf16)

    ids = doc[pl.ds(hi, 1), :].astype(f32)
    rows8 = jnp.where(lax.broadcasted_iota(jnp.int32, (8, 512), 0) == 0, ids, 0.0)
    doc_col = dot_over(rows8.astype(bf16), jnp.ones((8, 128), bf16))
    begin_one = jnp.sum(jnp.where(ids < 0.5, 1.0, 0.0), axis=-1, keepdims=True)
    begin_two = jnp.sum(jnp.where(ids < 1.5, 1.0, 0.0), axis=-1, keepdims=True)
    begin = jnp.where(doc_col > 1.5, begin_two, jnp.where(doc_col > 0.5, begin_one, 0.0))
    place = lax.broadcasted_iota(jnp.int32, (512, 128), 0).astype(f32) - begin
    turns = (lane & 31).astype(f32) * (2.0 / HD)
    angles = place * jnp.exp(turns * -math.log(160000.0))
    cosine[...] = jnp.cos(angles)
    sine[...] = jnp.where(low, -jnp.sin(angles), jnp.sin(angles))
    inverse_all[...] = doc_col
    for j in range(2):
        bias[local[j], :] = jnp.where(inverse_all[own[j], 0:1] == ids, 0.0, -1e30)

    def tile_up(g):
        def arrive(n, _):
            there = sb[g].at[owner(g, lax.rem(z + 8 - n, 8) * 2, 2)]
            remote(there, there, z_s.at[g, n], z_r.at[g, n], device(x, y, lax.rem(z + n, 8), c)).wait()
            return 0

        lax.fori_loop(1, 8, arrive, 0)
        sf[g][...] = sb[g][...].astype(f32)
        for p in range(2):
            for r in range(3):
                for t in range(MANY[g]):
                    line = (r * 2 + p) * MANY[g] + t
                    w[r, x, y, :, cols(g, c, p, t * 128, 128)] = sf[g][
                        pl.ds(line, 16, stride=SIZE[g]), :
                    ].astype(bf16)

    def one_step(g):
        return (
            Ring(x, along_x, lambda i, h: w.at[:, i, y, :, cols(g, c, 0, *CUT[g][h])],
                 ring_s.at[4 * g], ring_r.at[4 * g], None),
            Ring(y, along_y, lambda i, h: w.at[:, x, i, :, cols(g, c, 1, *CUT[g][h])],
                 ring_s.at[4 * g + 1], ring_r.at[4 * g + 1], None),
        )

    def two_step(g):
        return (
            Ring(y, along_y, lambda i, h: w.at[:, pl.ds(2 * h, 2), i, :, cols(g, c, 0)],
                 ring_s.at[4 * g + 2], ring_r.at[4 * g + 2], None),
            Ring(x, along_x, lambda i, h: w.at[:, i, pl.ds(2 * h, 2), :, cols(g, c, 1)],
                 ring_s.at[4 * g + 3], ring_r.at[4 * g + 3], None),
        )

    def piece(ref, p, i, at):
        return ref.at[:, :, i, :, at] if p == 0 else ref.at[:, i, :, :, at]

    handed = []

    def hand(g, ring, p, n, i):
        at = piece(w, p, i, cols(g, c, p))
        copy = remote(at, at, core_s.at[g, p, n], core_r.at[g, p, n], sib)
        copy.start()
        handed.append(copy)

    def taken(g, rings):
        for p in range(2):
            ring = rings[p]
            for n, i in enumerate((ring.me, ring.left, ring.right, ring.far)):
                at = piece(w, p, i, cols(g, 1 - c, p))
                remote(at, at, core_s.at[g, p, n], core_r.at[g, p, n], sib).wait_recv()

    def enter(b):
        rows = pl.ds(pl.multiple_of(b * 128, 128), 128)
        tokens = dot(xs[b], inner[...])
        tok_in[rows, :] = tokens.astype(bf16)
        normed, inverse = normalize(tokens)
        normed_all[rows, :] = normed
        inverse_all[rows, :] = jnp.broadcast_to(inverse, (128, 128))

    a_one, b_one, a_two, b_two = one_step(0), one_step(1), two_step(0), two_step(1)
    tile_up(0)
    for ring in a_one:
        ring.begin()
    tile_up(1)
    for ring in b_one:
        ring.begin()
    for ring in a_one:
        ring.forward()
    for ring in a_one:
        ring.near()
        ring.last()
    for ring in a_two:
        ring.begin()
    for p in range(2):
        hand(0, a_two[p], p, 0, a_two[p].me)
    for ring in b_one:
        ring.forward()
    enter(b_own)

    for n, at in enumerate((xs.at[b_far], gs.at[1 - hi])):
        remote(at, at, tok_s.at[n], tok_r.at[n], far).wait_recv()
    passed = remote(xs.at[b_far], xs.at[b_far], tok_s.at[3], tok_r.at[3], sib)
    passed.start()
    at = xs.at[2 * hi + 1 - c]
    remote(at, at, tok_s.at[2], tok_r.at[2], sib).wait_recv()
    for ring in b_one:
        ring.near()
        ring.last()
    for ring in a_two:
        ring.forward()
    for ring in b_two:
        ring.begin()
    for p in range(2):
        hand(1, b_two[p], p, 0, b_two[p].me)
    enter(b_far)
    for p in range(2):
        a_two[p].near()
        hand(0, a_two[p], p, 1, a_two[p].left)
        hand(0, a_two[p], p, 2, a_two[p].right)
    enter(2 * hi + 1 - c)
    for p in range(2):
        a_two[p].last()
        hand(0, a_two[p], p, 3, a_two[p].far)
    at = xs.at[2 * (1 - hi) + 1 - c]
    remote(at, at, tok_s.at[3], tok_r.at[3], sib).wait_recv()
    enter(2 * (1 - hi) + 1 - c)
    for j in range(2):
        top[local[j], :] = dot(gs[j], inner[...]).astype(bf16)
    top_t[...] = top[...].T
    taken(0, a_two)

    def wide(at):
        return w[:, :, :, :, at].reshape(D, at.size)

    def row_tile(n, at):
        return w[n, :, :, :, at].reshape(256, at.size)

    def put(at, value):
        d_w[:, :, :, :, at] = value.astype(bf16).reshape(3, 4, 4, 16, at.size)

    def turn(a, rows, sign):
        swap = jnp.where(low, pltpu.roll(a, 96, 1), pltpu.roll(a, 32, 1))
        return a * cosine[rows, :] + swap * (sign * sine[rows, :])

    pick = (
        lax.broadcasted_iota(jnp.int32, (8, 128), 0) == lax.broadcasted_iota(jnp.int32, (8, 128), 1)
    ).astype(f32).astype(bf16)
    gains = dot_rows(pick, wide(pl.ds(0, 128)))
    gain_one, gain_two = gains[0:1], gains[1:2]

    def scale(rows):
        in_all[rows, :] = (normed_all[rows, :] * gain_one).astype(bf16)

    tiles(4, 128, scale)

    def project(n):
        kk = dot(in_all[...], wide(shifted(n, 896)))
        k[:, n] = turn(kk, pl.ds(0, 512), 1.0).astype(bf16)
        v[:, n] = dot(in_all[...], wide(shifted(n, 1664))).astype(bf16)
        for j in range(2):
            q[local[j], n] = turn(dot(in_all[own[j], :], wide(shifted(n, 128))), own[j], 1.0).astype(bf16)

    tiles(6, 128, project)
    for ring in b_two:
        ring.forward()

    def attend(n, _):
        at = pl.ds(pl.multiple_of(n * 128, 128), 128)
        q2, k2, v2 = q[:, at], k[:, at], v[:, at]
        parts = []
        for h in range(2):
            score = dot_rows(jnp.where(heads[h], q2, jnp.zeros_like(q2)), k2) * 0.125 + bias[...]
            raised = jnp.exp(score - jnp.max(score, axis=-1, keepdims=True))
            prob = (raised * (1.0 / jnp.sum(raised, axis=-1, keepdims=True))).astype(bf16)
            soft[2 * n + h] = prob
            parts.append(dot(prob, v2))
        att[:, at] = jnp.where(heads[0], parts[0], parts[1]).astype(bf16)
        return 0

    lax.fori_loop(0, 3, attend, 0)
    for p in range(2):
        b_two[p].near()
        hand(1, b_two[p], p, 1, b_two[p].left)
        hand(1, b_two[p], p, 2, b_two[p].right)
    lax.fori_loop(3, 6, attend, 0)
    for p in range(2):
        b_two[p].last()
        hand(1, b_two[p], p, 3, b_two[p].far)
    taken(1, b_two)

    def leave(n, _):
        first_part[:, pl.ds(pl.multiple_of(n * 256, 256), 256)] = dot_rows(att[...], row_tile(n, pl.ds(2432, 768)))
        return 0

    lax.fori_loop(0, 3, leave, 0)
    inverse_two = []
    for j in range(2):
        residual = tok_in[own[j], :].astype(f32) + first_part[local[j], :]
        normed, inverse = normalize(residual)
        normed_two[local[j], :] = normed
        inverse_two.append(inverse)
        in_two[local[j], :] = (normed * gain_two).astype(bf16)

    def feed(n):
        gate = dot(in_two[...], wide(shifted(n, 3200)))
        up = dot(in_two[...], wide(shifted(n, 4352)))
        back = dot(top[...], wide(shifted(n, 5504)))
        cdf = 0.5 * (1.0 + lax.erf(gate * 0.7071067811865476))
        slope = cdf + gate * (jnp.exp(-0.5 * gate * gate) * 0.3989422804014327)
        act = gate * cdf
        hidden[:, n] = (act * up).astype(bf16)
        d_pre[:, n] = (back * up * slope).astype(bf16)
        d_pre[:, shifted(n, 1152)] = (back * act).astype(bf16)

    tiles(9, 128, feed)

    def finish(n, _):
        at = pl.ds(pl.multiple_of(n * 256, 256), 256)
        out_low[:, at] = (first_part[:, at] + dot_rows(hidden[...], row_tile(n, pl.ds(5504, 1152)))).astype(bf16)
        d_two[:, at] = dot_rows(d_pre[...], row_tile(n, pl.ds(3200, 2304)))
        return 0

    lax.fori_loop(0, 3, finish, 0)
    for j in range(2):
        grad, normed = d_two[local[j], :], normed_two[local[j], :]
        back = norm_back(grad * gain_two, normed, inverse_two[j])
        back_two[local[j], :] = back
        resid[local[j], :] = (top[local[j], :].astype(f32) + back).astype(bf16)

    in_two_t[...] = in_two[...].T
    resid_t[...] = resid[...].T

    def weights_o(n):
        put(shifted(n, 2432), dot(resid_t[...], att[:, n]))

    def weights_in(n):
        put(shifted(n, 3200), dot(in_two_t[...], d_pre[:, n]))

    def weights_down(n):
        put(shifted(n, 5504), dot(top_t[...], hidden[:, n]))

    tiles(3, 256, weights_o)
    tiles(9, 256, weights_in)
    tiles(3, 384, weights_down)

    land2, land1 = (land2_a, land2_b), (land1_a, land1_b)

    def back_two_step(g):
        return (
            Reduce(y, along_y, lambda i, h: d_w.at[:, 2 * h : 2 * h + 2, i, :, cols(g, c, 0)],
                   lambda s, h: land2[g].at[0, s], back_s.at[4 * g + 2], back_r.at[4 * g + 2]),
            Reduce(x, along_x, lambda i, h: d_w.at[:, i, 2 * h : 2 * h + 2, :, cols(g, c, 1)],
                   lambda s, h: land2[g].at[1, s], back_s.at[4 * g + 3], back_r.at[4 * g + 3]),
        )

    def back_one_step(g):
        return (
            Reduce(x, along_x, lambda i, h: d_w.at[:, i, y, :, cols(g, c, 0, *CUT[g][h])],
                   lambda s, h: land1[g].at[0, s, :, :, pl.ds(0, CUT[g][h][1])],
                   back_s.at[4 * g], back_r.at[4 * g]),
            Reduce(y, along_y, lambda i, h: d_w.at[:, x, i, :, cols(g, c, 1, *CUT[g][h])],
                   lambda s, h: land1[g].at[1, s, :, :, pl.ds(0, CUT[g][h][1])],
                   back_s.at[4 * g + 1], back_r.at[4 * g + 1]),
        )

    u_two, t_two, u_one, t_one = back_two_step(0), back_two_step(1), back_one_step(0), back_one_step(1)
    halves = {}

    def kept(g, p):
        return pl.ds(g * 1280 + p * WIDE[g], WIDE[g])

    def send_halves(g, rings):
        for n in range(4):
            for p in range(2):
                ring = rings[p]
                i = (ring.far, ring.right, ring.left, ring.me)[n]
                halves[g, p, n] = remote(
                    piece(d_w, p, i, cols(g, 1 - c, p)), piece(half, p, i, kept(g, p)),
                    half_s.at[g, p, n], half_r.at[g, p, n], sib,
                )
                halves[g, p, n].start()

    def chip_sum(g, rings, p, n):
        halves[g, p, n].wait_recv()
        ring = rings[p]
        i = (ring.far, ring.right, ring.left, ring.me)[n]
        add_into(piece(d_w, p, i, cols(g, c, p)), piece(half, p, i, kept(g, p)))

    send_halves(1, t_two)
    for j in range(2):
        d_out[j] = dot_rows(out_low[local[j], :], inner[...]).astype(bf16)
    give_out = remote(d_out.at[1 - hi], o_out.at[hi], ret_s.at[2], ret_r.at[2], far)
    give_out.start()
    keep_out = pltpu.make_async_copy(d_out.at[hi], o_out.at[hi], keep_s.at[0])
    keep_out.start()

    def toward(n):
        d_att[:, n] = dot(resid[...], wide(shifted(n, 2432))).astype(bf16)

    tiles(3, 256, toward)

    def behind(n, _):
        at = pl.ds(pl.multiple_of(n * 128, 128), 128)
        q2, k2, v2, a2 = q[:, at], k[:, at], v[:, at], d_att[:, at]
        both = a2.astype(f32) * att[:, at].astype(f32)
        dq, dk, dv = [], [], []
        for h in range(2):
            prob = soft[2 * n + h]
            delta = jnp.sum(jnp.where(heads[h], both, 0.0), axis=-1, keepdims=True)
            lift = dot_rows(jnp.where(heads[h], a2, jnp.zeros_like(a2)), v2)
            grad = (prob.astype(f32) * ((lift - delta) * 0.125)).astype(bf16)
            dq.append(dot(grad, k2))
            dk.append(dot_over(grad, q2))
            dv.append(dot_over(prob, a2))
        pick_head = lambda two: jnp.where(heads[0], two[0], two[1])
        dq = pick_head(dq)
        for j in range(2):
            d_q[local[j], at] = turn(dq[j * 128 : (j + 1) * 128], own[j], -1.0).astype(bf16)
        d_kv[:, at] = turn(pick_head(dk), pl.ds(0, 512), -1.0).astype(bf16)
        d_kv[:, shifted(at, 768)] = pick_head(dv).astype(bf16)
        return 0

    lax.fori_loop(0, 1, behind, 0)
    for p in range(2):
        chip_sum(1, t_two, p, 0)
        t_two[p].one()
    lax.fori_loop(1, 2, behind, 0)
    for p in range(2):
        chip_sum(1, t_two, p, 1)
        t_two[p].two()
        chip_sum(1, t_two, p, 2)
        t_two[p].three()
    lax.fori_loop(2, 4, behind, 0)
    for p in range(2):
        t_two[p].pass_right()
        t_two[p].pass_left()
    lax.fori_loop(4, 6, behind, 0)
    for p in range(2):
        chip_sum(1, t_two, p, 3)

    def through(n, _):
        at = pl.ds(pl.multiple_of(n * 256, 256), 256)
        d_one[:, at] = dot_rows(d_kv[...], row_tile(n, pl.ds(896, 1536)))
        for j in range(2):
            d_one[own[j], at] = d_one[own[j], at] + dot_rows(d_q[local[j], :], row_tile(n, pl.ds(128, 768)))
        return 0

    lax.fori_loop(0, 3, through, 0)
    gain_part = dot_over(
        (d_two[...] * normed_two[...]).astype(bf16),
        jnp.broadcast_to((lane == 1).astype(f32).astype(bf16), (256, 128)),
    )
    gain_part += dot_over(
        (d_one[...] * normed_all[...]).astype(bf16),
        jnp.broadcast_to((lane == 0).astype(f32).astype(bf16), (512, 128)),
    )
    put(pl.ds(0, 128), gain_part)
    in_all_t[...] = in_all[...].T
    for j in range(2):
        in_own_t[:, j * 128 : (j + 1) * 128] = in_all[own[j], :].T

    def weights_q(n):
        put(shifted(n, 128), dot(in_own_t[...], d_q[:, n]))

    def weights_kv(n):
        put(shifted(n, 896), dot(in_all_t[...], d_kv[:, n]))

    tiles(3, 256, weights_q)
    tiles(6, 256, weights_kv)
    send_halves(0, u_two)

    def sum_three(to, one, two):
        def row(r, _):
            to[r] = (to[r].astype(f32) + one[r].astype(f32) + two[r].astype(f32)).astype(bf16)
            return 0

        lax.fori_loop(0, 3, row, 0)

    def settle(g, rings, then):
        for p in range(2):
            ring = rings[p]
            ring.landed()
            for h in range(2):
                sum_three(ring.block(ring.me, h), land2[g].at[p, 2 + h], land2[g].at[p, 4 + h])
            then[p].one()
            then[p].two()
            then[p].three()

    settle(1, t_two, t_one)
    for p in range(2):
        chip_sum(0, u_two, p, 0)
        u_two[p].one()
    for p in range(2):
        chip_sum(0, u_two, p, 1)
        u_two[p].two()
        chip_sum(0, u_two, p, 2)
        u_two[p].three()

    def back_one(rows):
        grad, normed = d_one[rows, :], normed_all[rows, :]
        d_one[rows, :] = norm_back(grad * gain_one, normed, inverse_all[rows, 0:1])

    tiles(4, 128, back_one)
    for j in range(2):
        d_one[own[j], :] = d_one[own[j], :] + back_two[local[j], :]

    def leave_rows(b, _):
        rows = pl.ds(pl.multiple_of(b * 128, 128), 128)
        d_tok[b] = dot_rows(d_one[rows, :].astype(bf16), inner[...]).astype(bf16)
        return 0

    lax.fori_loop(0, 4, leave_rows, 0)
    tok_pair = []
    for j in range(2):
        copy = remote(d_tok.at[2 * j + 1 - c], tok_half.at[j], ret_s.at[j], ret_r.at[j], sib)
        copy.start()
        tok_pair.append(copy)

    for p in range(2):
        u_two[p].pass_right()
        u_two[p].pass_left()
    for p in range(2):
        t_one[p].pass_right()
        t_one[p].pass_left()
    for p in range(2):
        chip_sum(0, u_two, p, 3)
    for j in range(2):
        tok_pair[j].wait_recv()
        tok_sum[j] = (d_tok[2 * j + c].astype(f32) + tok_half[j].astype(f32)).astype(bf16)
    give_tok = remote(tok_sum.at[1 - hi], g_out.at[hi], ret_s.at[3], ret_r.at[3], far)
    give_tok.start()
    keep_tok = pltpu.make_async_copy(tok_sum.at[hi], g_out.at[hi], keep_s.at[1])
    keep_tok.start()

    def lay_out(g, rings):
        sf[g][...] = jnp.zeros(sf[g].shape, f32)
        for p in range(2):
            rings[p].landed()
            for r in range(3):
                for h in range(2):
                    at, n = CUT[g][h]
                    total = d_w[r, x, y, :, cols(g, c, p, at, n)].astype(f32)
                    total += land1[g][p, 2 + h, r, :, 0:n].astype(f32)
                    total += land1[g][p, 4 + h, r, :, 0:n].astype(f32)
                    for t in range(n // 128):
                        line = (r * 2 + p) * MANY[g] + at // 128 + t
                        sf[g][pl.ds(line, 16, stride=SIZE[g]), :] = total[:, t * 128 : (t + 1) * 128]
        sb[g][...] = sf[g][...].astype(bf16)

        def push_back(n, _):
            to = lax.rem(z + n, 8)
            remote(
                sb[g].at[owner(g, to * 2, 2)], zbuf[g].at[n], y_s.at[g, n], y_r.at[g, n], device(x, y, to, c)
            ).start()
            return 0

        lax.fori_loop(1, 8, push_back, 0)
        res[g][...] = sf[g][owner(g, z * 2, 2), :]

    ends = []

    def total_up(g):
        def arrive_back(n, _):
            remote(
                sb[g].at[owner(g, z * 2, 2)], zbuf[g].at[n], y_s.at[g, n], y_r.at[g, n],
                device(x, y, lax.rem(z + n, 8), c),
            ).wait()
            res[g][...] = res[g][...] + zbuf[g][n].astype(f32)
            return 0

        lax.fori_loop(1, 8, arrive_back, 0)
        theirs = remote(
            res[g].at[owner(g, 1 - c)], r_out.at[c, part[g]], fin_s.at[g], fin_r.at[g], sib
        )
        theirs.start()
        ours = pltpu.make_async_copy(res[g].at[owner(g, c)], r_out.at[c, part[g]], keep_s.at[2 + g])
        ours.start()
        ends.append((theirs, ours))

    lay_out(1, t_one)
    settle(0, u_two, u_one)
    for p in range(2):
        u_one[p].pass_right()
        u_one[p].pass_left()
    total_up(1)
    lay_out(0, u_one)
    total_up(0)
    for ring in a_one + a_two + b_one + b_two + t_two + t_one + u_two + u_one:
        ring.sent()
    for copy in list(halves.values()) + handed + give + [passed] + tok_pair + [give_out, give_tok]:
        copy.wait_send()
    keep_out.wait()
    keep_tok.wait()
    remote(d_out.at[0], o_out.at[1 - hi], ret_s.at[2], ret_r.at[2], far).wait_recv()
    remote(tok_sum.at[0], g_out.at[1 - hi], ret_s.at[3], ret_r.at[3], far).wait_recv()
    for g in range(2):
        theirs, ours = ends[1 - g]
        ours.wait()
        theirs.wait_send()
        remote(
            res[g].at[owner(g, 0)], r_out.at[1 - c, part[g]], fin_s.at[g], fin_r.at[g], sib
        ).wait_recv()


def block(blk, tok, cot, doc):
    dma = pltpu.SemaphoreType.DMA
    vm = pltpu.VMEM
    return pl.pallas_call(
        block_kernel,
        out_shape=(
            jax.ShapeDtypeStruct((2, 80, 128), f32),
            jax.ShapeDtypeStruct((2, 128, D), bf16),
            jax.ShapeDtypeStruct((2, 128, D), bf16),
        ),
        in_specs=[pl.BlockSpec(memory_space=pltpu.VMEM)] * 4,
        out_specs=[pl.BlockSpec(memory_space=pl.ANY)] * 3,
        scratch_shapes=[
            vm((512, 128), bf16), vm((768, 128), bf16), vm((512, 128), f32), vm((768, 128), f32), vm((128, D), bf16), vm((128, D), bf16),
            vm((4, 128, D), bf16), vm((2, 128, D), bf16),
            vm((3, 4, 4, 16, NC), bf16), vm((3, 4, 4, 16, NC), bf16), vm((3, 4, 4, 16, NC // 2), bf16),
            vm((2, 6, 3, 2, 16, 640), bf16), vm((2, 6, 3, 2, 16, 1024), bf16),
            vm((2, 6, 3, 16, 384), bf16), vm((2, 6, 3, 16, 512), bf16),
            vm((8, 64, 128), bf16), vm((8, 96, 128), bf16), vm((64, 128), f32), vm((96, 128), f32),
            vm((2, 128, D), bf16), vm((4, 128, D), bf16), vm((2, 128, D), bf16), vm((2, 128, D), bf16),
            vm((512, 128), f32), vm((512, 128), f32),
            vm((D, D), bf16), vm((512, D), bf16), vm((512, D), f32), vm((512, 128), f32), vm((512, D), bf16),
            vm((256, D), bf16), vm((512, D), bf16), vm((512, D), bf16), vm((256, 512), f32),
            vm((12, 256, 512), bf16), vm((256, D), bf16), vm((256, D), f32),
            vm((256, D), f32), vm((256, D), bf16), vm((256, D), bf16), vm((256, FF), bf16),
            vm((256, 2 * FF), bf16), vm((256, D), f32), vm((256, D), f32), vm((256, D), bf16),
            vm((256, D), bf16), vm((256, D), bf16), vm((512, 1536), bf16), vm((512, D), f32),
            vm((D, 512), bf16), vm((D, 256), bf16), vm((D, 256), bf16), vm((D, 256), bf16),
            vm((D, 256), bf16), vm((256, D), bf16),
            dma((2,)), dma((2,)), dma((2, 8)), dma((2, 8)), dma((8, 6)), dma((8, 6)), dma((2, 2, 4)), dma((2, 2, 4)),
            dma((2,)), dma((4,)), dma((4,)),
            dma((2, 2, 4)), dma((2, 2, 4)), dma((8, 6)), dma((8, 6)), dma((2, 8)), dma((2, 8)),
            dma((2,)), dma((2,)), dma((4,)), dma((4,)), dma((4,)),
        ],
        compiler_params=pltpu.CompilerParams(
            collective_id=0, has_side_effects=True, vmem_limit_bytes=63 * 2**20
        ),
        name="layer",
    )(blk, tok, cot, doc)


def pack_rows(weights):
    rows = jnp.concatenate(weights, axis=1)
    one = rows[:, :2560].reshape(3, 2, 10, 128).transpose(1, 0, 2, 3).reshape(2, 30, 128)
    two = rows[:, 2560:].reshape(3, 2, 16, 128).transpose(1, 0, 2, 3).reshape(2, 48, 128)
    return jnp.concatenate([jnp.pad(one, ((0, 0), (0, 2), (0, 0))), two], axis=1)


def finish_kernel(rows, out, tok, block_input, cotangent, y_out, g_out, qkv, w_o, w_i, w_d, gains):
    y_out[...] = block_input[...] + out[...].astype(f32)
    g_out[...] = cotangent[...] + tok[...].astype(f32)

    @pl.when(pl.program_id(0) == 0)
    def _():
        for t in range(52):
            core, line, step = (t // 10, t % 10, 10) if t < 20 else ((t - 20) // 16, 32 + (t - 20) % 16, 16)
            to, first = ((gains, 0), (qkv, 1), (w_o, 19), (w_i, 25), (w_d, 43))[
                sum(t >= n for n in (1, 19, 25, 43))
            ]
            at = (t - first) * 128
            for r in range(3):
                to[r : r + 1, at : at + 128] = rows[core, line + r * step : line + r * step + 1, :]


def finish(rows, out, tok, block_input, cotangent):
    one = pl.BlockSpec((1, 128, D), lambda n: (n, 0, 0))
    fixed = lambda *shape: pl.BlockSpec(shape, lambda n: (0,) * len(shape))
    widths = (3 * D, D, 2 * FF, FF, 128)
    return pl.pallas_call(
        finish_kernel,
        grid=(2,),
        out_shape=[jax.ShapeDtypeStruct((2, 128, D), f32)] * 2
        + [jax.ShapeDtypeStruct((3, n), f32) for n in widths],
        in_specs=[fixed(2, 80, 128)] + [one] * 4,
        out_specs=[one] * 2 + [fixed(3, n) for n in widths],
        name="finish",
    )(rows, out, tok, block_input, cotangent)


def body(
    block_input, doc_ids, positions, w_qkv, w_out, w_in, w_down, gain_attn, gain_ffn, cotangent
):
    gains = jnp.pad(jnp.stack([gain_attn, gain_ffn], axis=1), ((0, 0), (0, 126)))
    blk = pack_rows((gains, w_qkv, w_out, w_in, w_down))
    rows, out, tok = block(blk, block_input, cotangent, doc_ids)
    y_out, g_out, d_qkv, d_o, d_in, d_down, d_gain = finish(rows, out, tok, block_input, cotangent)
    return y_out, g_out, d_qkv, d_o, d_in, d_down, d_gain[:, 0], d_gain[:, 1]


def solution(mesh):
    split = P(("dp", "seq"), None)
    both = P("dp", "seq", None)
    return jax.shard_map(
        body,
        mesh=mesh,
        in_specs=(both, P("dp", None), P("dp", "seq"), split, split, split, split,
                  P(("dp", "seq")), P(("dp", "seq")), both),
        out_specs=(both, both, split, split, split, split, P(("dp", "seq")), P(("dp", "seq"))),
        check_vma=False,
    )
```
